512 devices in a mesh: row: 32 (over z, x), col: 16 (over y, core).
Axes of the slice: x: 4, y: 8, z: 8, core: 2. Of those that a mesh axis runs over, the one named last changes fastest.
Arguments:
- panel: float32 [9216, 256], P(('row', 'col')), may hold values from -60 to 636, as said below
- trailing: float32 [9216, 9216], P('row', 'col'), may hold values from -9 to 9
Outputs:
- updated: float32 [9216, 9216], P('row', 'col')
The draws below stay inside these ranges and needn't reach their ends.
Inputs may be any that keep to these rules, and one draw needn't show every extreme that they name: The panel's first 256 rows carry a positive diagonal between 288 and 576 on top of the other entries.
All inputs are finite; a program needn't handle non-finite values.
Results may differ from the reference program's by a relative error of at most 0.00017.
Values sent between devices are 32-bit elements; how exact they have to be, the bound alone decides.
No kernel may reach another device: no remote copies, remote signals or barrier semaphores. Data moves between devices by JAX's collectives and lax.ppermute only.
A program may use at most 64 MiB of HBM per device.

```python
import jax
import jax.numpy as jnp
from jax import lax

M = 9216
NB = 256


def draw_panel(key, part):
    keys = jax.random.split(jax.random.fold_in(key, 11), 3)
    scales = jnp.exp(jax.random.uniform(keys[0], (M, 1), jnp.float32) * jnp.log(10.0))
    noise = jnp.clip(jax.random.normal(keys[1], (M, NB), jnp.float32), -6.0, 6.0)
    diagonal = jax.random.uniform(keys[2], (NB,), jnp.float32, M / 32.0, M / 16.0)
    planted = jnp.concatenate([jnp.diag(diagonal), jnp.zeros((M - NB, NB), jnp.float32)], 0)
    return noise * scales + planted


def draw_trailing(key, part):
    inner_key = jax.random.fold_in(key, 23)
    base = jnp.clip(jax.random.normal(inner_key, (M, M), jnp.float32), -6.0, 6.0)
    return (base + base.T) * 0.70710678


def setup_inputs(seed: int = 0) -> dict:
    arg_keys = jax.random.split(jax.random.key(seed), 3)
    panel = draw_panel(jax.random.fold_in(arg_keys[2], 71), 0)
    trailing = draw_trailing(jax.random.fold_in(arg_keys[2], 71), 0)
    return {"panel": panel, "trailing": trailing}


def matmul(left, right):
    return jnp.dot(left.astype(jnp.float32), right.astype(jnp.float32), precision=lax.Precision.HIGHEST, preferred_element_type=jnp.float32)

def reference(panel, trailing):
    gram = lax.dot_general(panel.astype(jnp.float32), panel.astype(jnp.float32), (((0,), (0,)), ((), ())), precision=lax.Precision.HIGHEST, preferred_element_type=jnp.float32)
    top = panel[:NB]
    lower = jnp.linalg.cholesky(gram)
    basis = jax.scipy.linalg.solve_triangular(lower, panel.T, lower=True).T
    corner = jax.scipy.linalg.solve_triangular(lower, top.T, lower=True).T
    ident = jnp.eye(NB, dtype=jnp.float32)
    tmat = jnp.linalg.solve(ident + corner, ident)
    reflector = basis + jnp.concatenate([ident, jnp.zeros((M - NB, NB), jnp.float32)], 0)
    product = matmul(trailing, reflector)
    xmat = matmul(product, tmat)
    inner = lax.dot_general(reflector.astype(jnp.float32), xmat.astype(jnp.float32), (((0,), (0,)), ((), ())), precision=lax.Precision.HIGHEST, preferred_element_type=jnp.float32)
    small = matmul(tmat.T, inner)
    zmat = xmat - 0.5 * matmul(reflector, small)
    left = jnp.concatenate([zmat, reflector], 1)
    right = jnp.concatenate([reflector, zmat], 1)
    update = lax.dot_general(left.astype(jnp.float32), right.astype(jnp.float32), (((1,), (1,)), ((), ())), precision=lax.Precision.HIGHEST, preferred_element_type=jnp.float32)
    return trailing - update
```

```python
import functools

import jax
import jax.numpy as jnp
import numpy as np
from jax import lax
from jax.experimental import pallas as pl
from jax.experimental.pallas import tpu as pltpu
from jax.sharding import Mesh
from jax.sharding import PartitionSpec as P

HIGHEST = lax.Precision.HIGHEST
EVERY = ("z", "x", "y", "core")
COL = ("y", "core")
ROW = ("x", "z")

def tdot(a, b):
    return lax.dot_general(a, b, (((0,), (0,)), ((), ())), precision=HIGHEST, preferred_element_type=jnp.float32)


def dot(a, b):
    return lax.dot_general(a, b, (((1,), (0,)), ((), ())), precision=HIGHEST, preferred_element_type=jnp.float32)


def chol_step(panel, rows, block_col, step):
    pivot_col = panel[0][:, block_col + step : block_col + step + 1]
    scale = lax.rsqrt(pivot_col[step : step + 1, :])
    factor = jnp.where(rows > step, pivot_col * scale, 0.0)
    out = []
    for part in panel:
        row = part[step : step + 1, :] * scale
        out.append(jnp.where(rows == step, row, part - factor * row))
    return out


def inv_step(panel, rows, block_col, step):
    pivot_col = panel[0][:, block_col + step : block_col + step + 1]
    scale = 1.0 / pivot_col[step : step + 1, :]
    factor = jnp.where(rows == step, 0.0, pivot_col)
    out = []
    for part in panel:
        row = part[step : step + 1, :] * scale
        out.append(jnp.where(rows == step, row, part - factor * row))
    return out


def factor_body(block, gram_ref, top_ref, upper_ref, kmat_ref, schur, linv, mleft):
    n = gram_ref.shape[0]
    count = n // block
    schur[...] = gram_ref[...]
    mleft[...] = top_ref[...]
    row_ids = lax.broadcasted_iota(jnp.int32, (n, n), 0)
    col_ids = lax.broadcasted_iota(jnp.int32, (n, n), 1)
    linv[...] = jnp.where(row_ids == col_ids, 1.0, 0.0).astype(jnp.float32)
    kmat_ref[...] = jnp.zeros((n, n), jnp.float32)
    rows = lax.broadcasted_iota(jnp.int32, (block, 1), 0)
    brow = lax.broadcasted_iota(jnp.int32, (block, n), 0)
    bcol = lax.broadcasted_iota(jnp.int32, (block, n), 1)
    pending = None
    for k in range(count + 1):
        at = k * block
        prev = at - block
        if k < count:
            here = pl.ds(at, block)
            chol = [schur[here, :], linv[here, :]]
        if k > 0:
            before = pl.ds(prev, block)
            gj = [mleft[before, :] + pending[0], kmat_ref[before, :] + pending[1]]
        for step in range(block):
            if k < count:
                chol = chol_step(chol, rows, at, step)
            if k > 0:
                gj = inv_step(gj, rows, prev, step)
        if k < count:
            upper = jnp.where(bcol >= brow + at, chol[0], 0.0)
            upper_ref[here, :] = upper
            linv[here, :] = chol[1]
            if k + 1 < count:
                rest = pl.ds(at + block, n - at - block)
                right = upper[:, at + block :]
                schur[rest, :] = schur[rest, :] - tdot(right, upper)
                linv[rest, :] = linv[rest, :] - tdot(right, chol[1])
        if k > 0:
            mleft[before, :] = gj[0]
            kmat_ref[before, :] = gj[1]
            for lo, hi in ((0, prev), (at, n)):
                if hi > lo:
                    other = pl.ds(lo, hi - lo)
                    left = mleft[other, prev:at]
                    if hi > at:
                        mleft[other, :] = mleft[other, :] - dot(left, gj[0])
                    else:
                        mleft[other, :] = mleft[other, :] - dot(left, gj[0])
                    kmat_ref[other, :] = kmat_ref[other, :] - dot(left, gj[1])
        if k < count:
            pending = (upper, chol[1])


def factor(gram, top, block=32):
    n = gram.shape[0]
    shape = jax.ShapeDtypeStruct((n, n), jnp.float32)
    return pl.pallas_call(
        functools.partial(factor_body, block),
        out_shape=(shape, shape),
        in_specs=[pl.BlockSpec(memory_space=pltpu.VMEM)] * 2,
        out_specs=(pl.BlockSpec(memory_space=pltpu.VMEM),) * 2,
        scratch_shapes=[pltpu.VMEM((n, n), jnp.float32)] * 3,
        cost_estimate=pl.CostEstimate(flops=200000000, bytes_accessed=1000000, transcendentals=512),
        name="factor",
    )(gram, top)


def fold_owner(rows, cols):
    pairs = []
    for piece in range(rows * cols):
        owner = piece % rows
        target = (owner % (rows // 4)) * 4 + owner // (rows // 4)
        pairs.append((piece, target * cols + piece // rows))
    return pairs


def share_row(piece):
    depth, width = lax.axis_size("z"), lax.axis_size("x")
    ring = lax.all_to_all(jnp.broadcast_to(piece, (depth, *piece.shape)), "z", 0, 0)
    full = lax.all_to_all(jnp.broadcast_to(ring, (width, *ring.shape)), "x", 0, 0)
    return full.reshape(width * depth, *piece.shape)


def on_device(panel, trailing):
    n_row = lax.axis_size("z") * lax.axis_size("x")
    n_col = lax.axis_size("y") * lax.axis_size("core")
    piece, width = panel.shape
    row_at = lax.axis_index("z") * lax.axis_size("x") + lax.axis_index("x")
    col_at = lax.axis_index("y") * lax.axis_size("core") + lax.axis_index("core")
    moves = fold_owner(n_row, n_col)
    row_rows, col_rows = piece * n_col, piece * n_row
    g_rows = width // n_row
    c_rows = width // n_col

    p_piece = lax.ppermute(panel, EVERY, moves)
    p_row = lax.all_gather(panel, COL, axis=0, tiled=True)
    gram_part = tdot(p_row, p_row).reshape(n_row, g_rows, width)
    top_part = p_row[:width].reshape(n_row, g_rows, width)
    got = lax.all_to_all(jnp.concatenate([gram_part, top_part], 1), ROW, 0, 0)
    gram_piece = jnp.sum(got[:, :g_rows], 0)
    top_piece = got[0, g_rows:]
    shared = share_row(jnp.concatenate([gram_piece, top_piece, p_piece], 0))
    gram = shared[:, :g_rows].reshape(width, width)
    top = shared[:, g_rows : 2 * g_rows].reshape(width, width)
    p_col = shared[:, 2 * g_rows :].reshape(col_rows, width)

    upper, kmat = factor(gram, top)
    first_row = jnp.where(row_at == 0, upper, 0.0)
    first_col = jnp.where(col_at == 0, upper, 0.0)
    v_row = p_row + jnp.pad(first_row, ((0, row_rows - width), (0, 0)))
    v_col = p_col + jnp.pad(first_col, ((0, col_rows - width), (0, 0)))

    y_part = dot(trailing, v_col).reshape(n_col, piece, width)
    y_own = jnp.sum(lax.all_to_all(y_part, COL, 0, 0), 0)
    y_piece = lax.ppermute(y_own, EVERY, moves)
    y_col = share_row(y_piece).reshape(col_rows, width)
    c_part = tdot(v_col, y_col).reshape(n_col, c_rows, width)
    c_own = jnp.sum(lax.all_to_all(c_part, COL, 0, 0), 0)
    both = lax.all_gather(jnp.concatenate([c_own, y_own], 0), COL, axis=0)
    core = both[:, :c_rows].reshape(width, width)
    y_row = both[:, c_rows:].reshape(row_rows, width)

    left = jnp.concatenate([dot(y_row, kmat), v_row], 1)
    inner = y_col - dot(v_col, tdot(kmat, core))
    right = jnp.concatenate([v_col, dot(inner, kmat)], 1)
    update = lax.dot_general(
        left, right, (((1,), (1,)), ((), ())), precision=HIGHEST, preferred_element_type=jnp.float32
    )
    return trailing - update


def solution(mesh):
    grid = Mesh(np.asarray(mesh.devices).reshape(8, 4, 8, 2), EVERY)
    return jax.shard_map(
        on_device,
        mesh=grid,
        in_specs=(P(EVERY, None), P(("z", "x"), COL)),
        out_specs=P(("z", "x"), COL),
        check_vma=False,
    )
```

```python
import functools

import jax
import jax.numpy as jnp
import numpy as np
from jax import lax
from jax.experimental import pallas as pl
from jax.experimental.pallas import tpu as pltpu
from jax.sharding import Mesh
from jax.sharding import PartitionSpec as P


HIGHEST = lax.Precision.HIGHEST
HIGH = lax.Precision.HIGH
DEPTH, WIDTH = 8, 4
EVERY = ("z", "x", "y", "core")
COL = ("y", "core")
ROW = ("x", "z")

SUB, LANE = 8, 128


def tdot(a, b, precision=HIGHEST):
    return lax.dot_general(
        a, b, (((0,), (0,)), ((), ())), precision=precision, preferred_element_type=jnp.float32
    )


def dot(a, b, precision=HIGHEST):
    return jnp.dot(a, b, precision=precision, preferred_element_type=jnp.float32)


def load_tiles(refs, at, block):
    out = []
    for ref in refs:
        for lane in range(0, ref.shape[1], LANE):
            out.append([ref[at + t : at + t + SUB, lane : lane + LANE] for t in range(0, block, SUB)])
    return out


def spread_lane(tile, lane):
    return jnp.broadcast_to(tile[:, lane : lane + 1], (SUB, LANE))


def spread_row(tile, row):
    return jnp.broadcast_to(tile[row : row + 1, :], (SUB, LANE))


def chol_group(parts, group, at, sub_ids):
    part, lane = divmod(at + group * SUB, LANE)
    count = len(parts[0])
    cols = [spread_lane(parts[part][group], lane + k) for k in range(SUB)]
    entry = [[spread_row(cols[k], i) if i >= k else None for k in range(SUB)] for i in range(SUB)]
    below = [[spread_lane(parts[part][t], lane + k) for k in range(SUB)] for t in range(group + 1, count)]
    rows = [[spread_row(p[group], k) for k in range(SUB)] for p in parts]
    for k in range(SUB):
        scale = lax.rsqrt(entry[k][k])
        for i in range(k + 1, SUB):
            entry[i][k] = entry[i][k] * scale
        for j in range(k + 1, SUB):
            for i in range(j, SUB):
                entry[i][j] = entry[i][j] - entry[i][k] * entry[j][k]
        for line in below:
            line[k] = line[k] * scale
            for j in range(k + 1, SUB):
                line[j] = line[j] - line[k] * entry[j][k]
        for row in rows:
            row[k] = row[k] * scale
            for j in range(k + 1, SUB):
                row[j] = row[j] - entry[j][k] * row[k]
    for p, row in zip(parts, rows):
        tile = row[0]
        for k in range(1, SUB):
            tile = jnp.where(sub_ids == k, row[k], tile)
        p[group] = tile
        for t, line in zip(range(group + 1, count), below):
            for k in range(SUB):
                p[t] = p[t] - line[k] * row[k]


def inv_group(parts, group, at, sub_ids):
    part, lane = divmod(at + group * SUB, LANE)
    count = len(parts[0])
    cols = [spread_lane(parts[part][group], lane + k) for k in range(SUB)]
    entry = [[spread_row(cols[k], i) for k in range(SUB)] for i in range(SUB)]
    other = [t for t in range(count) if t != group]
    side = [[spread_lane(parts[part][t], lane + k) for k in range(SUB)] for t in other]
    rows = [[spread_row(p[group], k) for k in range(SUB)] for p in parts]
    for k in range(SUB):
        scale = 1.0 / entry[k][k]
        for j in range(k + 1, SUB):
            entry[k][j] = entry[k][j] * scale
        for row in rows:
            row[k] = row[k] * scale
        for i in range(SUB):
            if i != k:
                for j in range(k + 1, SUB):
                    entry[i][j] = entry[i][j] - entry[i][k] * entry[k][j]
                for row in rows:
                    row[i] = row[i] - entry[i][k] * row[k]
    for p, row in zip(parts, rows):
        tile = row[0]
        for k in range(1, SUB):
            tile = jnp.where(sub_ids == k, row[k], tile)
        p[group] = tile
        for t, line in zip(other, side):
            for k in range(SUB):
                p[t] = p[t] - line[k] * row[k]


def join(parts):
    return jnp.concatenate([jnp.concatenate(p, 0) for p in parts], 1)


def chol_body(block, gram_ref, upper_ref, linv_ref, schur):
    n = gram_ref.shape[0]
    half = n // LANE
    schur[...] = gram_ref[...]
    row_ids = lax.broadcasted_iota(jnp.int32, (n, n), 0)
    col_ids = lax.broadcasted_iota(jnp.int32, (n, n), 1)
    linv_ref[...] = jnp.where(row_ids == col_ids, 1.0, 0.0).astype(jnp.float32)
    sub_ids = lax.broadcasted_iota(jnp.int32, (SUB, LANE), 0)
    brow = lax.broadcasted_iota(jnp.int32, (block, n), 0)
    bcol = lax.broadcasted_iota(jnp.int32, (block, n), 1)
    for at in range(0, n, block):
        here = pl.ds(at, block)
        parts = load_tiles((schur, linv_ref), at, block)
        for group in range(block // SUB):
            chol_group(parts, group, at, sub_ids)
        upper = jnp.where(bcol >= brow + at, join(parts[:half]), 0.0)
        lower = join(parts[half:])
        upper_ref[here, :] = upper
        linv_ref[here, :] = lower
        if at + block < n:
            rest = pl.ds(at + block, n - at - block)
            right = upper[:, at + block :]
            schur[rest, :] = schur[rest, :] - tdot(right, upper)
            linv_ref[rest, :] = linv_ref[rest, :] - tdot(right, lower)


def inv_body(block, upper_ref, linv_ref, top_ref, kmat_ref, left):
    n = top_ref.shape[0]
    half = n // LANE
    left[...] = top_ref[...] + upper_ref[...]
    kmat_ref[...] = linv_ref[...]
    sub_ids = lax.broadcasted_iota(jnp.int32, (SUB, LANE), 0)
    for at in range(0, n, block):
        here = pl.ds(at, block)
        parts = load_tiles((left, kmat_ref), at, block)
        for group in range(block // SUB):
            inv_group(parts, group, at, sub_ids)
        keep = join(parts[:half])
        out = join(parts[half:])
        left[here, :] = keep
        kmat_ref[here, :] = out
        for lo, hi in ((at + block, n), (0, at)):
            if hi > lo:
                other = pl.ds(lo, hi - lo)
                column = left[other, at : at + block]
                if at + block < n:
                    left[other, :] = left[other, :] - dot(column, keep)
                kmat_ref[other, :] = kmat_ref[other, :] - dot(column, out)


def local_call(body, outs, scratch, block, *args):
    n = args[0].shape[0]
    shape = jax.ShapeDtypeStruct((n, n), jnp.float32)
    vmem = pl.BlockSpec(memory_space=pltpu.VMEM)
    return pl.pallas_call(
        functools.partial(body, block),
        out_shape=(shape,) * outs,
        in_specs=[vmem] * len(args),
        out_specs=(vmem,) * outs,
        scratch_shapes=[pltpu.VMEM((n, n), jnp.float32)] * scratch,
        cost_estimate=pl.CostEstimate(
            flops=16_000_000_000, bytes_accessed=4 * n * n * (outs + len(args)), transcendentals=n
        ),
    )(*args)


def fold_moves(rows, cols):
    pairs = []
    for piece in range(rows * cols):
        owner = piece % rows
        target = (owner % DEPTH) * WIDTH + owner // DEPTH
        pairs.append((piece, target * cols + piece // rows))
    return pairs


def on_device(panel, trailing):
    n_row = lax.axis_size("z") * lax.axis_size("x")
    n_col = lax.axis_size("y") * lax.axis_size("core")
    piece, width = panel.shape
    row_at = lax.axis_index("z") * lax.axis_size("x") + lax.axis_index("x")
    col_at = lax.axis_index("y") * lax.axis_size("core") + lax.axis_index("core")
    moves = fold_moves(n_row, n_col)
    back = [(target, source) for source, target in moves]
    row_rows, col_rows = piece * n_col, piece * n_row
    c_rows, g_rows = width // n_col, width // n_row

    def share_row(part):
        copies = jnp.broadcast_to(part, (n_row, *part.shape))
        return lax.all_to_all(copies, ROW, 0, 0)

    def share_twice(part):
        ring = lax.all_to_all(jnp.broadcast_to(part, (DEPTH, *part.shape)), "z", 0, 0)
        full = lax.all_to_all(jnp.broadcast_to(ring, (WIDTH, *ring.shape)), "x", 0, 0)
        return full.reshape(n_row, *part.shape)

    def sum_twice(stack):
        stack = stack.reshape(WIDTH, DEPTH, *stack.shape[1:])
        stack = jnp.sum(lax.all_to_all(stack, "x", 0, 0), 0)
        return jnp.sum(lax.all_to_all(stack, "z", 0, 0), 0)

    p_far = lax.ppermute(panel, EVERY, moves)
    p_row = lax.all_gather(panel, COL, axis=0, tiled=True)
    first = row_at == 0
    stacked = [
        tdot(trailing, p_row, HIGH).reshape(n_row, piece, width),
        jnp.where(first, trailing[:width], 0.0).T.reshape(n_row, piece, width),
        tdot(p_row, p_row).reshape(n_row, g_rows, width),
        jnp.where(first, p_row[:width], 0.0).reshape(n_row, g_rows, width),
    ]
    moved = sum_twice(jnp.concatenate(stacked, 1))
    at = 2 * piece
    ap_far, ae_far = moved[:piece], moved[piece:at]
    both = share_row(moved[at:])
    gram = both[:, :g_rows].reshape(width, width)
    top = both[:, g_rows:].reshape(width, width)

    upper, linv = local_call(chol_body, 2, 1, 64, gram)
    (kmat,) = local_call(inv_body, 1, 1, 64, upper, linv, top)

    y_far = ap_far + dot(ae_far, upper, HIGH)
    both = share_twice(jnp.concatenate([y_far, p_far], 0))
    y_col = both[:, :piece].reshape(col_rows, width)
    p_col = both[:, piece:].reshape(col_rows, width)
    y_own = lax.ppermute(y_far, EVERY, back)
    first_row = jnp.where(first, upper, 0.0)
    first_col = jnp.where(col_at == 0, upper, 0.0)
    v_row = p_row + jnp.pad(first_row, ((0, row_rows - width), (0, 0)))
    v_col = p_col + jnp.pad(first_col, ((0, col_rows - width), (0, 0)))
    c_part = tdot(v_col, y_col, HIGH).reshape(n_col, c_rows, width)
    c_part = lax.all_to_all(c_part, COL, 0, 0)
    last = lax.all_gather(jnp.concatenate([jnp.sum(c_part, 0), y_own], 0), COL, axis=0)
    core = last[:, :c_rows].reshape(width, width)
    y_row = last[:, c_rows:].reshape(row_rows, width)

    left = jnp.concatenate([dot(y_row, kmat, HIGH), v_row], 1)
    inner = y_col - dot(v_col, tdot(kmat, core, HIGH), HIGH)
    right = jnp.concatenate([v_col, dot(inner, kmat, HIGH)], 1)
    update = lax.dot_general(
        left, right, (((1,), (1,)), ((), ())), precision=HIGH, preferred_element_type=jnp.float32
    )
    return trailing - update


def solution(mesh):
    grid = Mesh(np.asarray(mesh.devices).reshape(DEPTH, WIDTH, 8, 2), EVERY)
    return jax.shard_map(
        on_device,
        mesh=grid,
        in_specs=(P(EVERY, None), P(("z", "x"), COL)),
        out_specs=P(("z", "x"), COL),
        check_vma=False,
    )
```

```python
import functools

import jax
import jax.numpy as jnp
import numpy as np
from jax import lax
from jax.experimental import pallas as pl
from jax.experimental.pallas import tpu as pltpu
from jax.sharding import Mesh
from jax.sharding import PartitionSpec as P


HIGHEST = lax.Precision.HIGHEST
HIGH = lax.Precision.HIGH
DEPTH, WIDTH = 8, 4
EVERY = ("z", "x", "y", "core")
COL = ("y", "core")
ROW = ("x", "z")

SUB, LANE = 8, 128


def tdot(a, b, precision=HIGHEST):
    return lax.dot_general(
        a, b, (((0,), (0,)), ((), ())), precision=precision, preferred_element_type=jnp.float32
    )


def dot(a, b, precision=HIGHEST):
    return jnp.dot(a, b, precision=precision, preferred_element_type=jnp.float32)


def load_tiles(ref, at, block, lanes):
    return [
        [ref[at + t : at + t + SUB, lane : lane + LANE] for t in range(0, block, SUB)]
        for lane in lanes
    ]


def spread_lane(tile, lane):
    return jnp.broadcast_to(tile[:, lane : lane + 1], (SUB, LANE))


def spread_row(tile, row):
    return jnp.broadcast_to(tile[row : row + 1, :], (SUB, LANE))


def chol_group(parts, group, at, sub_ids):
    part, lane = 0, (at + group * SUB) % LANE
    count = len(parts[0])
    cols = [spread_lane(parts[part][group], lane + k) for k in range(SUB)]
    entry = [[spread_row(cols[k], i) if i >= k else None for k in range(SUB)] for i in range(SUB)]
    below = [[spread_lane(parts[part][t], lane + k) for k in range(SUB)] for t in range(group + 1, count)]
    rows = [[spread_row(p[group], k) for k in range(SUB)] for p in parts]
    for k in range(SUB):
        scale = lax.rsqrt(entry[k][k])
        for i in range(k + 1, SUB):
            entry[i][k] = entry[i][k] * scale
        for j in range(k + 1, SUB):
            for i in range(j, SUB):
                entry[i][j] = entry[i][j] - entry[i][k] * entry[j][k]
        for line in below:
            line[k] = line[k] * scale
            for j in range(k + 1, SUB):
                line[j] = line[j] - line[k] * entry[j][k]
        for row in rows:
            row[k] = row[k] * scale
            for j in range(k + 1, SUB):
                row[j] = row[j] - entry[j][k] * row[k]
    for p, row in zip(parts, rows):
        tile = row[0]
        for k in range(1, SUB):
            tile = jnp.where(sub_ids == k, row[k], tile)
        p[group] = tile
        for t, line in zip(range(group + 1, count), below):
            for k in range(SUB):
                p[t] = p[t] - line[k] * row[k]


def inv_group(parts, group, at, sub_ids):
    part, lane = 0, (at + group * SUB) % LANE
    count = len(parts[0])
    cols = [spread_lane(parts[part][group], lane + k) for k in range(SUB)]
    entry = [[spread_row(cols[k], i) for k in range(SUB)] for i in range(SUB)]
    other = [t for t in range(count) if t != group]
    side = [[spread_lane(parts[part][t], lane + k) for k in range(SUB)] for t in other]
    rows = [[spread_row(p[group], k) for k in range(SUB)] for p in parts]
    for k in range(SUB):
        scale = 1.0 / entry[k][k]
        for j in range(k + 1, SUB):
            entry[k][j] = entry[k][j] * scale
        for row in rows:
            row[k] = row[k] * scale
        for i in range(SUB):
            if i != k:
                for j in range(k + 1, SUB):
                    entry[i][j] = entry[i][j] - entry[i][k] * entry[k][j]
                for row in rows:
                    row[i] = row[i] - entry[i][k] * row[k]
    for p, row in zip(parts, rows):
        tile = row[0]
        for k in range(1, SUB):
            tile = jnp.where(sub_ids == k, row[k], tile)
        p[group] = tile
        for t, line in zip(other, side):
            for k in range(SUB):
                p[t] = p[t] - line[k] * row[k]


def join(parts):
    return jnp.concatenate([jnp.concatenate(p, 0) for p in parts], 1)


def chol_body(block, shared_ref, ap_ref, ae_ref, p_ref, upper_ref, copies_ref, schur):
    n = upper_ref.shape[0]
    piece = ap_ref.shape[0]
    schur[...] = shared_ref[:, : n // shared_ref.shape[0], :].reshape(n, n)
    upper_ref[...] = jnp.zeros((n, n), jnp.float32)
    sub_ids = lax.broadcasted_iota(jnp.int32, (SUB, LANE), 0)
    for at in range(0, n, block):
        here = pl.ds(at, block)
        base = at // LANE * LANE
        parts = load_tiles(schur, at, block, range(base, n, LANE))
        for group in range(block // SUB):
            chol_group(parts, group, at, sub_ids)
        rows = lax.broadcasted_iota(jnp.int32, (block, n - base), 0) + at
        cols = lax.broadcasted_iota(jnp.int32, (block, n - base), 1) + base
        upper = jnp.where(cols >= rows, join(parts), 0.0)
        upper_ref[here, base:] = upper
        after = at + block
        if after < n:
            rest = pl.ds(after, n - after)
            keep = after // LANE * LANE
            update = tdot(upper[:, after - base :], upper[:, keep - base :])
            schur[rest, keep:] = schur[rest, keep:] - update
    y_far = ap_ref[...] + dot(ae_ref[...], upper_ref[...])
    for peer in range(copies_ref.shape[0]):
        copies_ref[peer, :piece, :] = y_far
        copies_ref[peer, piece:, :] = p_ref[...]


def inv_body(block, shared_ref, upper_ref, kmat_ref, left):
    n = upper_ref.shape[0]
    g_rows = n // shared_ref.shape[0]
    gram = shared_ref[:, :g_rows, :].reshape(n, n)
    top = shared_ref[:, g_rows:, :].reshape(n, n)
    left[...] = gram + tdot(upper_ref[...], top)
    row_ids = lax.broadcasted_iota(jnp.int32, (n, n), 0)
    col_ids = lax.broadcasted_iota(jnp.int32, (n, n), 1)
    kmat_ref[...] = jnp.where(row_ids == col_ids, 1.0, 0.0).astype(jnp.float32)
    sub_ids = lax.broadcasted_iota(jnp.int32, (SUB, LANE), 0)
    for at in range(0, n, block):
        here = pl.ds(at, block)
        base = at // LANE * LANE
        done = base + LANE
        parts = load_tiles(left, at, block, range(base, n, LANE))
        split = len(parts)
        parts += load_tiles(kmat_ref, at, block, range(0, done, LANE))
        for group in range(block // SUB):
            inv_group(parts, group, at, sub_ids)
        keep = join(parts[:split])
        out = join(parts[split:])
        left[here, base:] = keep
        kmat_ref[here, :done] = out
        for lo, hi in ((at + block, n), (0, at)):
            if hi > lo:
                other = pl.ds(lo, hi - lo)
                column = left[other, at : at + block]
                if at + block < n:
                    left[other, base:] = left[other, base:] - dot(column, keep)
                kmat_ref[other, :done] = kmat_ref[other, :done] - dot(column, out)


def pair_body(both_ref, first_ref, v_ref, y_ref, c_ref):
    count, twice, _ = both_ref.shape
    piece = twice // 2
    for k in range(count):
        y_ref[k * piece : (k + 1) * piece, :] = both_ref[k, :piece, :]
        v_ref[k * piece : (k + 1) * piece, :] = both_ref[k, piece:, :]
    n = first_ref.shape[0]
    v_ref[:n, :] = v_ref[:n, :] + first_ref[...]
    c_ref[...] = tdot(v_ref[...], y_ref[...])


def local_call(body, outs, scratch, flops, *args):
    vmem = pl.BlockSpec(memory_space=pltpu.VMEM)
    shapes = tuple(jax.ShapeDtypeStruct(out, jnp.float32) for out in outs)
    moved = sum(4 * int(np.prod(shape)) for shape in outs + [arg.shape for arg in args])
    return pl.pallas_call(
        body,
        out_shape=shapes,
        in_specs=[vmem] * len(args),
        out_specs=(vmem,) * len(outs),
        scratch_shapes=[pltpu.VMEM(shape, jnp.float32) for shape in scratch],
        cost_estimate=pl.CostEstimate(flops=flops, bytes_accessed=moved, transcendentals=256),
    )(*args)


def fold_moves(rows, cols):
    pairs = []
    for piece in range(rows * cols):
        owner = piece % rows
        target = (owner % DEPTH) * WIDTH + owner // DEPTH
        pairs.append((piece, target * cols + piece // rows))
    return pairs


def on_device(panel, trailing):
    n_row = lax.axis_size("z") * lax.axis_size("x")
    n_col = lax.axis_size("y") * lax.axis_size("core")
    piece, width = panel.shape
    row_at = lax.axis_index("z") * lax.axis_size("x") + lax.axis_index("x")
    col_at = lax.axis_index("y") * lax.axis_size("core") + lax.axis_index("core")
    moves = fold_moves(n_row, n_col)
    back = [(target, source) for source, target in moves]
    row_rows, col_rows = piece * n_col, piece * n_row
    c_rows, g_rows = width // n_col, width // n_row

    def share_row(part):
        copies = jnp.broadcast_to(part, (n_row, *part.shape))
        return lax.all_to_all(copies, ROW, 0, 0)

    def sum_twice(stack):
        stack = stack.reshape(WIDTH, DEPTH, *stack.shape[1:])
        stack = jnp.sum(lax.all_to_all(stack, "x", 0, 0), 0)
        return jnp.sum(lax.all_to_all(stack, "z", 0, 0), 0)

    p_far = lax.ppermute(panel, EVERY, moves)
    p_row = lax.all_gather(panel, COL, axis=0, tiled=True)
    first = row_at == 0
    stacked = [
        tdot(trailing, p_row, HIGH).reshape(n_row, piece, width),
        jnp.where(first, trailing[:width], 0.0).T.reshape(n_row, piece, width),
        tdot(p_row, p_row).reshape(n_row, g_rows, width),
        jnp.where(first, p_row[:width], 0.0).reshape(n_row, g_rows, width),
    ]
    moved = sum_twice(jnp.concatenate(stacked, 1))
    at = 2 * piece
    ap_far, ae_far = moved[:piece], moved[piece:at]
    shared = share_row(moved[at:])
    square = (width, width)
    upper, copies = local_call(
        functools.partial(chol_body, 64),
        [square, (DEPTH, at, width)],
        [square],
        10_000_000_000,
        *(shared, ap_far, ae_far, p_far),
    )
    (kmat,) = local_call(
        functools.partial(inv_body, 64), [square], [square], 14_000_000_000, shared, upper
    )

    ring = lax.all_to_all(copies, "z", 0, 0)
    both = lax.all_to_all(jnp.broadcast_to(ring, (WIDTH, *ring.shape)), "x", 0, 0)
    both = both.reshape(n_row, at, width)
    y_own = lax.ppermute(copies[0, :piece], EVERY, back)
    first_row = jnp.where(first, upper, 0.0)
    first_col = jnp.where(col_at == 0, upper, 0.0)
    v_row = p_row + jnp.pad(first_row, ((0, row_rows - width), (0, 0)))
    v_col, y_col, c_part = local_call(
        pair_body, [(col_rows, width)] * 2 + [square], [], 2_000_000_000, both, first_col
    )
    c_part = lax.all_to_all(c_part.reshape(n_col, c_rows, width), COL, 0, 0)
    last = lax.all_gather(jnp.concatenate([jnp.sum(c_part, 0), y_own], 0), COL, axis=0)
    core = last[:, :c_rows].reshape(width, width)
    y_row = last[:, c_rows:].reshape(row_rows, width)

    left = jnp.concatenate([dot(y_row, kmat, HIGH), v_row], 1)
    inner = y_col - dot(v_col, tdot(kmat, core, HIGH), HIGH)
    right = jnp.concatenate([v_col, dot(inner, kmat, HIGH)], 1)
    update = lax.dot_general(
        left, right, (((1,), (1,)), ((), ())), precision=HIGH, preferred_element_type=jnp.float32
    )
    return trailing - update


def solution(mesh):
    grid = Mesh(np.asarray(mesh.devices).reshape(DEPTH, WIDTH, 8, 2), EVERY)
    return jax.shard_map(
        on_device,
        mesh=grid,
        in_specs=(P(EVERY, None), P(("z", "x"), COL)),
        out_specs=P(("z", "x"), COL),
        check_vma=False,
    )
```

```python
import functools

import jax
import jax.numpy as jnp
import numpy as np
from jax import lax
from jax.experimental import pallas as pl
from jax.experimental.pallas import tpu as pltpu
from jax.sharding import Mesh
from jax.sharding import PartitionSpec as P


HIGHEST = lax.Precision.HIGHEST
HIGH = lax.Precision.HIGH
DEPTH, WIDTH = 8, 4
EVERY = ("z", "x", "y", "core")
COL = ("y", "core")
ROW = ("x", "z")

SUB, LANE = 8, 128


def tdot(a, b, precision=HIGHEST):
    return lax.dot_general(
        a, b, (((0,), (0,)), ((), ())), precision=precision, preferred_element_type=jnp.float32
    )


def dot(a, b, precision=HIGHEST):
    return jnp.dot(a, b, precision=precision, preferred_element_type=jnp.float32)


def load_tiles(ref, at, block, lanes):
    return [
        [ref[at + t : at + t + SUB, lane : lane + LANE] for t in range(0, block, SUB)]
        for lane in lanes
    ]


def spread_lane(tile, lane):
    return jnp.broadcast_to(tile[:, lane : lane + 1], (SUB, LANE))


def spread_row(tile, row):
    return jnp.broadcast_to(tile[row : row + 1, :], (SUB, LANE))


def chol_group(parts, group, at, sub_ids):
    part, lane = 0, (at + group * SUB) % LANE
    count = len(parts[0])
    cols = [spread_lane(parts[part][group], lane + k) for k in range(SUB)]
    entry = [[spread_row(cols[k], i) if i >= k else None for k in range(SUB)] for i in range(SUB)]
    below = [[spread_lane(parts[part][t], lane + k) for k in range(SUB)] for t in range(group + 1, count)]
    rows = [[spread_row(p[group], k) for k in range(SUB)] for p in parts]
    for k in range(SUB):
        scale = lax.rsqrt(entry[k][k])
        for i in range(k + 1, SUB):
            entry[i][k] = entry[i][k] * scale
        for j in range(k + 1, SUB):
            for i in range(j, SUB):
                entry[i][j] = entry[i][j] - entry[i][k] * entry[j][k]
        for line in below:
            line[k] = line[k] * scale
            for j in range(k + 1, SUB):
                line[j] = line[j] - line[k] * entry[j][k]
        for row in rows:
            row[k] = row[k] * scale
            for j in range(k + 1, SUB):
                row[j] = row[j] - entry[j][k] * row[k]
    for p, row in zip(parts, rows):
        tile = row[0]
        for k in range(1, SUB):
            tile = jnp.where(sub_ids == k, row[k], tile)
        p[group] = tile
        for t, line in zip(range(group + 1, count), below):
            for k in range(SUB):
                p[t] = p[t] - line[k] * row[k]


def inv_group(parts, group, at, sub_ids):
    part, lane = 0, (at + group * SUB) % LANE
    count = len(parts[0])
    cols = [spread_lane(parts[part][group], lane + k) for k in range(SUB)]
    entry = [[spread_row(cols[k], i) for k in range(SUB)] for i in range(SUB)]
    other = [t for t in range(count) if t != group]
    side = [[spread_lane(parts[part][t], lane + k) for k in range(SUB)] for t in other]
    rows = [[spread_row(p[group], k) for k in range(SUB)] for p in parts]
    for k in range(SUB):
        scale = 1.0 / entry[k][k]
        for j in range(k + 1, SUB):
            entry[k][j] = entry[k][j] * scale
        for row in rows:
            row[k] = row[k] * scale
        for i in range(SUB):
            if i != k:
                for j in range(k + 1, SUB):
                    entry[i][j] = entry[i][j] - entry[i][k] * entry[k][j]
                for row in rows:
                    row[i] = row[i] - entry[i][k] * row[k]
    for p, row in zip(parts, rows):
        tile = row[0]
        for k in range(1, SUB):
            tile = jnp.where(sub_ids == k, row[k], tile)
        p[group] = tile
        for t, line in zip(other, side):
            for k in range(SUB):
                p[t] = p[t] - line[k] * row[k]


def join(parts):
    return jnp.concatenate([jnp.concatenate(p, 0) for p in parts], 1)


def chol_body(block, shared_ref, ap_ref, ae_ref, p_ref, upper_ref, copies_ref, schur):
    n = upper_ref.shape[0]
    piece = ap_ref.shape[0]
    schur[...] = shared_ref[:, : n // shared_ref.shape[0], :].reshape(n, n)
    upper_ref[...] = jnp.zeros((n, n), jnp.float32)
    sub_ids = lax.broadcasted_iota(jnp.int32, (SUB, LANE), 0)
    for at in range(0, n, block):
        here = pl.ds(at, block)
        base = at // LANE * LANE
        parts = load_tiles(schur, at, block, range(base, n, LANE))
        for group in range(block // SUB):
            chol_group(parts, group, at, sub_ids)
        rows = lax.broadcasted_iota(jnp.int32, (block, n - base), 0) + at
        cols = lax.broadcasted_iota(jnp.int32, (block, n - base), 1) + base
        upper = jnp.where(cols >= rows, join(parts), 0.0)
        upper_ref[here, base:] = upper
        after = at + block
        if after < n:
            rest = pl.ds(after, n - after)
            keep = after // LANE * LANE
            update = tdot(upper[:, after - base :], upper[:, keep - base :])
            schur[rest, keep:] = schur[rest, keep:] - update
    y_far = ap_ref[...] + dot(ae_ref[...], upper_ref[...])
    for peer in range(copies_ref.shape[0]):
        copies_ref[peer, :piece, :] = y_far
        copies_ref[peer, piece:, :] = p_ref[...]


def inv_body(block, shared_ref, upper_ref, kmat_ref, left):
    n = upper_ref.shape[0]
    g_rows = n // shared_ref.shape[0]
    gram = shared_ref[:, :g_rows, :].reshape(n, n)
    top = shared_ref[:, g_rows:, :].reshape(n, n)
    left[...] = gram + tdot(upper_ref[...], top)
    row_ids = lax.broadcasted_iota(jnp.int32, (n, n), 0)
    col_ids = lax.broadcasted_iota(jnp.int32, (n, n), 1)
    kmat_ref[...] = jnp.where(row_ids == col_ids, 1.0, 0.0).astype(jnp.float32)
    sub_ids = lax.broadcasted_iota(jnp.int32, (SUB, LANE), 0)
    for at in range(0, n, block):
        here = pl.ds(at, block)
        base = at // LANE * LANE
        done = base + LANE
        parts = load_tiles(left, at, block, range(base, n, LANE))
        split = len(parts)
        parts += load_tiles(kmat_ref, at, block, range(0, done, LANE))
        for group in range(block // SUB):
            inv_group(parts, group, at, sub_ids)
        keep = join(parts[:split])
        out = join(parts[split:])
        left[here, base:] = keep
        kmat_ref[here, :done] = out
        for lo, hi in ((at + block, n), (0, at)):
            if hi > lo:
                other = pl.ds(lo, hi - lo)
                column = left[other, at : at + block]
                if at + block < n:
                    left[other, base:] = left[other, base:] - dot(column, keep)
                kmat_ref[other, :done] = kmat_ref[other, :done] - dot(column, out)


def pair_body(both_ref, first_ref, v_ref, y_ref, c_ref):
    groups, _, _ = both_ref.shape
    piece = y_ref.shape[0] // (groups * DEPTH)
    for k in range(groups * DEPTH):
        start = k % DEPTH * 2 * piece
        here = pl.ds(k * piece, piece)
        y_ref[here, :] = both_ref[k // DEPTH, start : start + piece, :]
        v_ref[here, :] = both_ref[k // DEPTH, start + piece : start + 2 * piece, :]
    n = first_ref.shape[0]
    v_ref[:n, :] = v_ref[:n, :] + first_ref[...]
    c_ref[...] = tdot(v_ref[...], y_ref[...])


def local_call(body, outs, scratch, flops, *args):
    vmem = pl.BlockSpec(memory_space=pltpu.VMEM)
    shapes = tuple(jax.ShapeDtypeStruct(out, jnp.float32) for out in outs)
    moved = sum(4 * int(np.prod(shape)) for shape in outs + [arg.shape for arg in args])
    return pl.pallas_call(
        body,
        out_shape=shapes,
        in_specs=[vmem] * len(args),
        out_specs=(vmem,) * len(outs),
        scratch_shapes=[pltpu.VMEM(shape, jnp.float32) for shape in scratch],
        cost_estimate=pl.CostEstimate(flops=flops, bytes_accessed=moved, transcendentals=256),
    )(*args)


def fold_moves(rows, cols):
    pairs = []
    for piece in range(rows * cols):
        owner = piece % rows
        target = (owner % DEPTH) * WIDTH + owner // DEPTH
        pairs.append((piece, target * cols + piece // rows))
    return pairs


def on_device(panel, trailing):
    n_row = lax.axis_size("z") * lax.axis_size("x")
    n_col = lax.axis_size("y") * lax.axis_size("core")
    piece, width = panel.shape
    row_at = lax.axis_index("z") * lax.axis_size("x") + lax.axis_index("x")
    col_at = lax.axis_index("y") * lax.axis_size("core") + lax.axis_index("core")
    moves = fold_moves(n_row, n_col)
    back = [(target, source) for source, target in moves]
    row_rows, col_rows = piece * n_col, piece * n_row
    c_rows, g_rows = width // n_col, width // n_row

    def share_row(part):
        copies = jnp.broadcast_to(part, (n_row, *part.shape))
        return lax.all_to_all(copies, ROW, 0, 0)

    def sum_twice(stack):
        stack = stack.reshape(WIDTH, DEPTH, *stack.shape[1:])
        stack = jnp.sum(lax.all_to_all(stack, "x", 0, 0), 0)
        return jnp.sum(lax.all_to_all(stack, "z", 0, 0), 0)

    p_far = lax.ppermute(panel, EVERY, moves)
    p_row = lax.all_gather(panel, COL, axis=0, tiled=True)
    first = row_at == 0
    stacked = [
        tdot(trailing, p_row, HIGH).reshape(n_row, piece, width),
        jnp.where(first, trailing[:width], 0.0).T.reshape(n_row, piece, width),
        tdot(p_row, p_row).reshape(n_row, g_rows, width),
        jnp.where(first, p_row[:width], 0.0).reshape(n_row, g_rows, width),
    ]
    moved = sum_twice(jnp.concatenate(stacked, 1))
    at = 2 * piece
    ap_far, ae_far = moved[:piece], moved[piece:at]
    shared = share_row(moved[at:])
    square = (width, width)
    upper, copies = local_call(
        functools.partial(chol_body, 64),
        [square, (DEPTH, at, width)],
        [square],
        10_000_000_000,
        *(shared, ap_far, ae_far, p_far),
    )
    (kmat,) = local_call(
        functools.partial(inv_body, 64), [square], [square], 14_000_000_000, shared, upper
    )

    ring = lax.all_to_all(copies, "z", 0, 0).reshape(DEPTH * at, width)
    both = lax.all_to_all(jnp.broadcast_to(ring, (WIDTH, *ring.shape)), "x", 0, 0)
    y_own = lax.ppermute(copies[0, :piece], EVERY, back)
    first_row = jnp.where(first, upper, 0.0)
    first_col = jnp.where(col_at == 0, upper, 0.0)
    v_row = p_row + jnp.pad(first_row, ((0, row_rows - width), (0, 0)))
    v_col, y_col, c_part = local_call(
        pair_body, [(col_rows, width)] * 2 + [square], [], 2_000_000_000, both, first_col
    )
    c_part = lax.all_to_all(c_part.reshape(n_col, c_rows, width), COL, 0, 0)
    last = lax.all_gather(jnp.concatenate([jnp.sum(c_part, 0), y_own], 0), COL, axis=0)
    core = last[:, :c_rows].reshape(width, width)
    y_row = last[:, c_rows:].reshape(row_rows, width)

    left = jnp.concatenate([dot(y_row, kmat, HIGH), v_row], 1)
    inner = y_col - dot(v_col, tdot(kmat, core, HIGH), HIGH)
    right = jnp.concatenate([v_col, dot(inner, kmat, HIGH)], 1)
    update = lax.dot_general(
        left, right, (((1,), (1,)), ((), ())), precision=HIGH, preferred_element_type=jnp.float32
    )
    return trailing - update


def solution(mesh):
    grid = Mesh(np.asarray(mesh.devices).reshape(DEPTH, WIDTH, 8, 2), EVERY)
    return jax.shard_map(
        on_device,
        mesh=grid,
        in_specs=(P(EVERY, None), P(("z", "x"), COL)),
        out_specs=P(("z", "x"), COL),
        check_vma=False,
    )
```
